32 devices in a mesh: days: 4 (over y, x), assets: 8 (over z, core).
Axes of the slice: x: 2, y: 2, z: 4, core: 2. Of those that a mesh axis runs over, the one named last changes fastest.
Arguments:
- factors: bfloat16 [768, 256], P('days'), may hold values from -6 to 6
- returns: bfloat16 [768, 16384], P('days', 'assets'), may hold values from -6 to 6
Outputs:
- loadings: float32 [256, 16384], P(None, 'assets')
- covariance: float32 [16384, 16384], P('assets', 'days')
The draws below stay inside these ranges and needn't reach their ends.
All inputs are finite; a program needn't handle non-finite values.
Results may differ from the reference program's by a relative error of at most 0.0036.
Values may be sent and summed in bfloat16 or wider, within the bound.
No kernel may reach another device: no remote copies, remote signals or barrier semaphores. Data moves between devices by JAX's collectives and lax.ppermute only.
A program may use at most 128 MiB of HBM per device.

```python
import jax
import jax.numpy as jnp
from jax import lax

K = 256
ASSETS = 16384
DAYS = 768


def block_scale(rng, dims, cuts, least, high):
    level, own = 1.0, jax.random.fold_in(rng, 6)
    for axis_at, shards_of in cuts:
        draws = jnp.exp(jax.random.uniform(jax.random.fold_in(own, axis_at), (shards_of,), jnp.float32, least / len(cuts), high / len(cuts)))
        level = level * jnp.repeat(draws, dims[axis_at] // shards_of).reshape([-1 if axis == axis_at else 1 for axis in range(len(dims))])
    return level


def centred(stream_key, dims, scale, limit, pieces=(), kind=jnp.bfloat16):
    entries = jax.random.normal(stream_key, dims, jnp.float32) * scale
    if len(pieces) > 0:
        entries = block_scale(stream_key, dims, pieces, -0.22, 0.18) * entries
    return jnp.clip(entries, min=-limit, max=limit).astype(kind)


def setup_inputs(seed: int = 0) -> dict:
    key_of = jax.random.split(jax.random.key(seed), 3)
    factors = centred(key_of[0], (DAYS, K), 1.0, 6.0, ((0, 4),))
    returns = centred(key_of[1], (DAYS, ASSETS), 1.0, 6.0, ((0, 4), (1, 8)))
    return dict(factors=factors, returns=returns)


def reference(factors, returns):
    gram = lax.dot_general(factors.astype(jnp.float32), factors.astype(jnp.float32), (((0,), (0,)), ((), ())), preferred_element_type=jnp.float32)
    cross = lax.dot_general(factors.astype(jnp.float32), returns.astype(jnp.float32), (((0,), (0,)), ((), ())), preferred_element_type=jnp.float32)
    lower = jnp.linalg.cholesky(gram)
    middle = lax.linalg.triangular_solve(lower, cross, left_side=True, lower=True)
    loadings = lax.linalg.triangular_solve(lower, middle, left_side=True, lower=True, transpose_a=True)
    fitted = jnp.dot(factors.astype(jnp.float32), loadings.astype(jnp.bfloat16).astype(jnp.float32), preferred_element_type=jnp.float32)
    residual = (returns.astype(jnp.float32) - fitted).astype(jnp.bfloat16)

    def block_rows(start):
        rows = lax.dynamic_slice_in_dim(residual, start, 1024, 1)
        return lax.dot_general(rows.astype(jnp.float32), residual.astype(jnp.float32), (((0,), (0,)), ((), ())), preferred_element_type=jnp.float32)
    width = residual.shape[1]
    step = min(1024, width)
    if step == 1024:
        starts = jnp.arange(0, width, 1024).astype(jnp.int32)
        covariance = lax.map(block_rows, starts).reshape(width, width)
    else:
        covariance = lax.dot_general(residual.astype(jnp.float32), residual.astype(jnp.float32), (((0,), (0,)), ((), ())), preferred_element_type=jnp.float32)
    covariance = covariance / residual.shape[0]
    return (loadings, covariance)
```

```python
import functools

import jax
import jax.numpy as jnp
from jax import lax
from jax.experimental import pallas as pl
from jax.experimental.pallas import tpu as pltpu
from jax.sharding import PartitionSpec as P

AXES = ("days", "assets")
NB = 32
INV_CALLS = 4
CHUNKS = (2, 1, 1)
BF, F32 = jnp.bfloat16, jnp.float32
HIGHEST = lax.Precision.HIGHEST


def dot(a, b, dims=((1,), (0,)), precision=None):
    return lax.dot_general(a, b, (dims, ((), ())), precision=precision, preferred_element_type=F32)


def cost(flops, nbytes):
    return pl.CostEstimate(flops=int(flops), bytes_accessed=int(nbytes), transcendentals=0)


def small_inverse(block):
    n = block.shape[0]
    row = lax.broadcasted_iota(jnp.int32, (n, n), 0)
    col = lax.broadcasted_iota(jnp.int32, (n, n), 1)
    for k in range(n):
        pivot = 1.0 / block[k : k + 1, k : k + 1]
        r = jnp.where(col[:1] == k, 1.0, block[k : k + 1, :]) * pivot
        c = jnp.where(row[:, :1] == k, -1.0, block[:, k : k + 1])
        block = jnp.where((row == k) | (col == k), 0.0, block) - c * r
    return block


def sweep(a, b):
    size = a.shape[0]
    lo, hi = b * NB, (b + 1) * NB
    row = lax.broadcasted_iota(jnp.int32, (size, size), 0)
    col = lax.broadcasted_iota(jnp.int32, (size, size), 1)
    inverse = small_inverse(a[lo:hi, lo:hi])
    across = dot(inverse, a[lo:hi, :], precision=HIGHEST)
    rows = lax.broadcasted_iota(jnp.int32, (size, NB), 0) - lo
    cols = lax.broadcasted_iota(jnp.int32, (size, NB), 1)
    down = jnp.where((rows >= 0) & (rows < NB), jnp.where(rows == cols, -1.0, 0.0), a[:, lo:hi])
    inside = ((row >= lo) & (row < hi)) | ((col >= lo) & (col < hi))
    a[...] = jnp.where(inside, 0.0, a[...]) - dot(down, across, precision=HIGHEST)
    a[:, lo:hi] = -dot(down, inverse, precision=HIGHEST)


def gram_kernel(n, order, *refs):
    pieces, full, gram = refs[:n], refs[n], refs[n + 1]
    depth = pieces[0].shape[0]
    for j in range(n):
        full[pl.ds(pl.multiple_of(order[j] * depth, depth), depth), :] = pieces[j][...]
    gram[...] = dot(full[...], full[...], ((0,), (0,)))


def sweep_kernel(blocks, a_ref, o_ref):
    o_ref[...] = a_ref[...]
    for b in blocks:
        sweep(o_ref, b)


def map_kernel(blocks, a_ref, f_ref, high, low, a):
    a[...] = a_ref[...]
    for b in blocks:
        sweep(a, b)
    h = dot(a[...], f_ref[...].astype(F32), ((1,), (1,)), precision=HIGHEST)
    top = h.astype(BF)
    high[...] = top
    low[...] = (h - top.astype(F32)).astype(BF)


def invert(order, pieces):
    n = len(pieces)
    depth, size = pieces[0].shape
    full, gram = pl.pallas_call(
        functools.partial(gram_kernel, n),
        in_specs=[pl.BlockSpec(memory_space=pltpu.SMEM)] + [pl.BlockSpec(memory_space=pltpu.VMEM)] * n,
        out_shape=[jax.ShapeDtypeStruct((n * depth, size), BF), jax.ShapeDtypeStruct((size, size), F32)],
        cost_estimate=cost(2 * n * depth * size * size, 4 * n * depth * size),
        name="gram",
    )(order, *pieces)
    count = size // NB
    each = -(-count // INV_CALLS)
    groups = [tuple(range(s, min(s + each, count))) for s in range(0, count, each)]
    work = cost(2.5e9, 8 * size * size)
    for group in groups[:-1]:
        gram = pl.pallas_call(
            functools.partial(sweep_kernel, group),
            out_shape=jax.ShapeDtypeStruct((size, size), F32),
            cost_estimate=work,
            name="sweep",
        )(gram)
    high, low = pl.pallas_call(
        functools.partial(map_kernel, groups[-1]),
        out_shape=[jax.ShapeDtypeStruct((size, n * depth), BF)] * 2,
        scratch_shapes=[pltpu.VMEM((size, size), F32)],
        cost_estimate=work,
        name="map",
    )(gram, full)
    return full, high, low


def residual_kernel(n, halves, with_loadings, order, *refs):
    tiles = pl.num_programs(0)
    count = n + 1 if halves else n
    pieces = refs[:count]
    high, low, factors = refs[count : count + 3]
    outs = refs[count + 3 : -1]
    y = refs[-1]
    depth = pieces[0].shape[0]

    def put(j, ref):
        y[pl.ds(pl.multiple_of(order[j] * depth, depth), depth), :] = ref[...]

    for j in range(n - 1 if halves else n):
        put(j, pieces[j])
    if halves:
        left = pl.program_id(0) < tiles // 2

        @pl.when(left)
        def _():
            put(n - 1, pieces[n - 1])

        @pl.when(jnp.logical_not(left))
        def _():
            put(n - 1, pieces[n])

    loadings = dot(high[...], y[...]) + dot(low[...], y[...])
    fitted = dot(factors[...], loadings.astype(BF))
    outs[0][...] = (y[...].astype(F32) - fitted).astype(BF)
    if with_loadings:
        outs[1][...] = loadings


def residuals(order, pieces, high, low, factors, width, with_loadings, halves=False, tile=512):
    n = len(pieces) - 1 if halves else len(pieces)
    depth = pieces[0].shape[0]
    size, days = high.shape
    tile = min(tile, width // 2 if halves else width)
    tiles = width // tile
    spec = pl.BlockSpec((depth, tile), lambda i, order: (0, i))
    specs = [spec] * n
    if halves:
        half = tiles // 2
        specs = specs[:-1] + [
            pl.BlockSpec((depth, tile), lambda i, order: (0, jnp.minimum(i, half - 1))),
            pl.BlockSpec((depth, tile), lambda i, order: (0, jnp.maximum(i - half, 0))),
        ]
    whole = lambda shape: pl.BlockSpec(shape, lambda i, order: (0, 0))
    out_specs = [pl.BlockSpec((days, tile), lambda i, order: (0, i))]
    out_shape = [jax.ShapeDtypeStruct((days, width), BF)]
    if with_loadings:
        out_specs.append(pl.BlockSpec((size, tile), lambda i, order: (0, i)))
        out_shape.append(jax.ShapeDtypeStruct((size, width), F32))
    return pl.pallas_call(
        functools.partial(residual_kernel, n, halves, with_loadings),
        grid_spec=pltpu.PrefetchScalarGridSpec(
            num_scalar_prefetch=1,
            grid=(tiles,),
            in_specs=specs + [whole((size, days))] * 2 + [whole((days, size))],
            out_specs=out_specs,
            scratch_shapes=[pltpu.VMEM((days, tile), BF)],
        ),
        out_shape=out_shape,
        cost_estimate=cost(6 * days * size * width, 4 * days * width),
        name="residual",
    )(order, *pieces, high, low, factors)


def covariance_kernel(scale, where, rows, cols, *refs):
    refs[-1][...] = dot(rows[...], cols[...], ((0,), (0,))) * scale


def covariance(held, rows, cols, start, total, days, tile=512):
    depth, height = rows.shape
    width = cols.shape[1]
    tile = min(tile, width)
    specs = [
        pl.BlockSpec((depth, height), lambda j, where: (0, 0)),
        pl.BlockSpec((depth, tile), lambda j, where: (0, j)),
    ]
    args = [rows, cols]
    aliases = {}
    if held is not None:
        specs.append(pl.BlockSpec(memory_space=pl.ANY))
        args.append(held)
        aliases = {3: 0}
    return pl.pallas_call(
        functools.partial(covariance_kernel, 1.0 / days),
        grid_spec=pltpu.PrefetchScalarGridSpec(
            num_scalar_prefetch=1,
            grid=(width // tile,),
            in_specs=specs,
            out_specs=pl.BlockSpec((height, tile), lambda j, where: (0, where[0] + j)),
        ),
        out_shape=jax.ShapeDtypeStruct((height, total), F32),
        input_output_aliases=aliases,
        cost_estimate=cost(2 * depth * height * width, 4 * height * width),
        name="covariance",
    )((start // tile).reshape(1).astype(jnp.int32), *args)


def per_device(nd, na, factors, returns):
    reps = na // nd
    nq = na // reps
    depth, width = returns.shape
    days = depth * nd
    xor = nd & (nd - 1) == 0

    def partner(d, j):
        return d ^ j if xor else (d + j) % nd

    def back(d, j):
        return d ^ j if xor else (d - j) % nd

    def move(x, target):
        pairs = []
        for d in range(nd):
            for a in range(na):
                to = target(d, a // reps, a % reps)
                if to is not None:
                    pairs.append((d * na + a, to[0] * na + to[1] * reps + to[2]))
        return lax.ppermute(x, AXES, pairs)

    def plane(x, j):
        return move(x, lambda d, q, c: (back(d, j), q, c))

    d = lax.axis_index("days")
    a = lax.axis_index("assets")
    q, c = a // reps, a % reps
    order = jnp.stack([partner(d, j) for j in range(nd)]).astype(jnp.int32)

    factor_pieces = [factors] + [plane(factors, j) for j in range(1, nd)]

    sizes = [width * s // sum(CHUNKS) for s in CHUNKS]
    starts = [sum(sizes[:i]) for i in range(len(sizes))]

    def along(own):
        up, down = {0: own}, {0: own}
        for s in range(1, nq):
            up[s] = move(up[s - 1], lambda d, q, c, s=s: (d, q + 1, c) if s - 1 <= q < nq - 1 else None)
            down[s] = move(down[s - 1], lambda d, q, c, s=s: (d, q - 1, c) if 0 < q <= nq - s else None)
        return up, down

    def pick(up, down, target):
        x = up[0]
        for s in range(1, nq):
            x = jnp.where(target == q + s, down[s], x)
            x = jnp.where(target == q - s, up[s], x)
        return x

    halves = nd == 4 and xor
    if halves:
        one, two = plane(returns, 1), plane(returns, 2)
        row_pieces = [returns, one, two, plane(one[:, : width // 2], 2), plane(two[:, width // 2 :], 1)]
    else:
        row_pieces = [returns] + [plane(returns, j) for j in range(1, nd)]

    chunk_pieces = []
    for start, size in zip(starts, sizes):
        up, down = along(returns[:, start : start + size])
        pieces = [pick(up, down, d)]
        for j in range(1, nd):
            pieces.append(plane(pick(up, down, order_back(d, j, nd, xor)), j))
        chunk_pieces.append(pieces)

    full, high, low = invert(order, factor_pieces)
    rows, loadings = residuals(order, row_pieces, high, low, full, width, True, halves)

    held = None
    total = reps * width
    for start, pieces in zip(starts, chunk_pieces):
        (cols,) = residuals(order, pieces, high, low, full, pieces[0].shape[1], False)
        for s in range(reps):
            if s == 0:
                part = cols
            else:
                part = move(cols, lambda d, q, c, s=s: (d, q, (c - s) % reps))
            at = ((c + s) % reps) * width + start
            held = covariance(held, rows, part, at, total, days)
    return loadings, held


def order_back(d, j, nd, xor):
    return d ^ j if xor else (d - j) % nd


def solution(mesh):
    nd, na = mesh.shape["days"], mesh.shape["assets"]
    return jax.shard_map(
        functools.partial(per_device, nd, na),
        mesh=mesh,
        in_specs=(P("days", None), P("days", "assets")),
        out_specs=(P(None, "assets"), P("assets", "days")),
        check_vma=False,
    )
```

```python
import functools

import jax
import jax.numpy as jnp
from jax import lax
from jax.experimental import pallas as pl
from jax.experimental.pallas import tpu as pltpu
from jax.sharding import PartitionSpec as P


AXES = ("days", "assets")
NB = 64
STEPS = 24
CHUNKS = (1, 1)
BF, F32 = jnp.bfloat16, jnp.float32
VMEM_ALL = 67043328
HIGHEST = lax.Precision.HIGHEST


def dot(a, b, dims=((1,), (0,)), precision=None):
    return lax.dot_general(a, b, (dims, ((), ())), precision=precision, preferred_element_type=F32)


def cost(flops, nbytes):
    return pl.CostEstimate(flops=int(flops), bytes_accessed=int(nbytes), transcendentals=0)


def small_inverse(block):
    n = block.shape[0]
    row = lax.broadcasted_iota(jnp.int32, (n, n), 0)
    col = lax.broadcasted_iota(jnp.int32, (n, n), 1)
    for k in range(n):
        pivot = 1.0 / block[k : k + 1, k : k + 1]
        r = jnp.where(col[:1] == k, 1.0, block[k : k + 1, :]) * pivot
        c = jnp.where(row[:, :1] == k, -1.0, block[:, k : k + 1])
        block = jnp.where((row == k) | (col == k), 0.0, block) - c * r
    return block


def sweep(a, b):
    size = a.shape[0]
    lo, hi = b * NB, (b + 1) * NB
    wide = lambda shape, axis: lax.broadcasted_iota(jnp.int32, shape, axis)
    inverse = small_inverse(a[lo:hi, lo:hi])
    across = wide((NB, size), 1) - lo
    unit = jnp.where(wide((NB, size), 0) == across, 1.0, 0.0)
    across = dot(inverse, jnp.where((across >= 0) & (across < NB), unit, a[lo:hi, :]), precision=HIGHEST)
    rows = wide((size, NB), 0) - lo
    unit = jnp.where(rows == wide((size, NB), 1), -1.0, 0.0)
    down = jnp.where((rows >= 0) & (rows < NB), unit, a[:, lo:hi])
    row, col = wide((size, size), 0), wide((size, size), 1)
    inside = ((row >= lo) & (row < hi)) | ((col >= lo) & (col < hi))
    a[...] = jnp.where(inside, 0.0, a[...]) - dot(down, across, precision=HIGHEST)


def split(a):
    high = a.astype(BF)
    return high, (a - high.astype(F32)).astype(BF)


def dot3(a, b):
    return dot(a[0], b[0]) + dot(a[0], b[1]) + dot(a[1], b[0])


def invert_kernel(n, order, *refs):
    pieces = refs[:n]
    full, high, low, gram, x = refs[n:]
    depth, size = pieces[0].shape
    for j in range(n):
        full[pl.ds(pl.multiple_of(order[j] * depth, depth), depth), :] = pieces[j][...]
    gram[...] = dot(full[...], full[...], ((0,), (0,)))

    parts = split(gram[...])
    row = lax.broadcasted_iota(jnp.int32, (size, size), 0)
    col = lax.broadcasted_iota(jnp.int32, (size, size), 1)
    eye = jnp.where(row == col, 1.0, 0.0)
    bound = jnp.max(jnp.sum(jnp.abs(gram[...]), axis=0, keepdims=True), axis=1, keepdims=True)
    x[...] = eye * (1.0 / bound)

    def step():
        at = split(x[...])
        rest = eye - dot3(parts, at)
        x[...] = x[...] + dot3(at, split(rest))
        return rest

    for _ in range(4):
        step()

    def body(carry):
        rest = step()
        return carry[0] + 1, jnp.sum(rest * rest)

    def going(carry):
        return (carry[0] < STEPS) & jnp.logical_not(carry[1] < 1e-4)

    _, error = lax.while_loop(going, body, (0, jnp.float32(1.0)))
    done = error < 1e-4

    @pl.when(done)
    def _():
        rest = eye - dot(gram[...], x[...], precision=HIGHEST)
        x[...] = x[...] + dot(x[...], rest, precision=HIGHEST)

    @pl.when(jnp.logical_not(done))
    def _():
        x[...] = gram[...]
        for b in range(size // NB):
            sweep(x, b)

    h = dot(x[...], full[...].astype(F32), ((1,), (1,)), precision=HIGHEST)
    high[...], low[...] = split(h)


def invert(order, pieces):
    n = len(pieces)
    depth, size = pieces[0].shape
    days = n * depth
    return pl.pallas_call(
        functools.partial(invert_kernel, n),
        in_specs=[pl.BlockSpec(memory_space=pltpu.SMEM)] + [pl.BlockSpec(memory_space=pltpu.VMEM)] * n,
        out_shape=[jax.ShapeDtypeStruct((days, size), BF)] + [jax.ShapeDtypeStruct((size, days), BF)] * 2,
        scratch_shapes=[pltpu.VMEM((size, size), F32)] * 2,
        cost_estimate=cost(2e10, 8 * days * size),
        compiler_params=pltpu.CompilerParams(vmem_limit_bytes=VMEM_ALL),
        name="gram",
    )(order, *pieces)


def residual_kernel(n, halves, with_loadings, order, *refs):
    tiles = pl.num_programs(0)
    count = n + 1 if halves else n
    pieces = refs[:count]
    high, low, factors = refs[count : count + 3]
    outs = refs[count + 3 : -1]
    y = refs[-1]
    depth = pieces[0].shape[0]

    def put(j, ref):
        y[pl.ds(pl.multiple_of(order[j] * depth, depth), depth), :] = ref[...]

    for j in range(n - 1 if halves else n):
        put(j, pieces[j])
    if halves:
        left = pl.program_id(0) < tiles // 2

        @pl.when(left)
        def _():
            put(n - 1, pieces[n - 1])

        @pl.when(jnp.logical_not(left))
        def _():
            put(n - 1, pieces[n])

    loadings = dot(high[...], y[...]) + dot(low[...], y[...])
    fitted = dot(factors[...], loadings.astype(BF))
    outs[0][...] = (y[...].astype(F32) - fitted).astype(BF)
    if with_loadings:
        outs[1][...] = loadings


def residuals(order, pieces, high, low, factors, width, with_loadings, halves=False, tile=512):
    n = len(pieces) - 1 if halves else len(pieces)
    depth = pieces[0].shape[0]
    size, days = high.shape
    tile = min(tile, width // 2 if halves else width)
    tiles = width // tile
    spec = pl.BlockSpec((depth, tile), lambda i, order: (0, i))
    specs = [spec] * n
    if halves:
        half = tiles // 2
        specs = specs[:-1] + [
            pl.BlockSpec((depth, tile), lambda i, order: (0, jnp.minimum(i, half - 1))),
            pl.BlockSpec((depth, tile), lambda i, order: (0, jnp.maximum(i - half, 0))),
        ]
    whole = lambda shape: pl.BlockSpec(shape, lambda i, order: (0, 0))
    out_specs = [pl.BlockSpec((days, tile), lambda i, order: (0, i))]
    out_shape = [jax.ShapeDtypeStruct((days, width), BF)]
    if with_loadings:
        out_specs.append(pl.BlockSpec((size, tile), lambda i, order: (0, i)))
        out_shape.append(jax.ShapeDtypeStruct((size, width), F32))
    return pl.pallas_call(
        functools.partial(residual_kernel, n, halves, with_loadings),
        grid_spec=pltpu.PrefetchScalarGridSpec(
            num_scalar_prefetch=1,
            grid=(tiles,),
            in_specs=specs + [whole((size, days))] * 2 + [whole((days, size))],
            out_specs=out_specs,
            scratch_shapes=[pltpu.VMEM((days, tile), BF)],
        ),
        out_shape=out_shape,
        cost_estimate=cost(6 * days * size * width, 4 * days * width),
        compiler_params=pltpu.CompilerParams(vmem_limit_bytes=VMEM_ALL),
        name="residual",
    )(order, *pieces, high, low, factors)


def covariance_kernel(scale, count, where, rows, *refs):
    out = refs[-1]
    step = pl.program_id(0)
    for k in range(count):
        @pl.when(step == k if count > 1 else step >= 0)
        def _():
            out[...] = dot(rows[...], refs[k][...], ((0,), (0,))) * scale


def covariance(held, rows, parts, starts, total, days, tile=512):
    depth, height = rows.shape
    width = parts[0].shape[1]
    tile = min(tile, width)
    count, tiles = len(parts), width // tile
    specs = [pl.BlockSpec((depth, height), lambda k, j, where: (0, 0))]
    for k in range(count):
        held_at = lambda s, j, where, k=k: (0, jnp.where(s == k, j, jnp.where(s < k, 0, tiles - 1)))
        specs.append(pl.BlockSpec((depth, tile), held_at))
    args = [rows, *parts]
    aliases = {}
    if held is not None:
        specs.append(pl.BlockSpec(memory_space=pl.ANY))
        args.append(held)
        aliases = {len(args): 0}
    return pl.pallas_call(
        functools.partial(covariance_kernel, 1.0 / days, count),
        grid_spec=pltpu.PrefetchScalarGridSpec(
            num_scalar_prefetch=1,
            grid=(count, tiles),
            in_specs=specs,
            out_specs=pl.BlockSpec((height, tile), lambda k, j, where: (0, where[k] + j)),
        ),
        out_shape=jax.ShapeDtypeStruct((height, total), F32),
        input_output_aliases=aliases,
        cost_estimate=cost(2 * depth * height * width * count, 4 * height * width * count),
        compiler_params=pltpu.CompilerParams(vmem_limit_bytes=VMEM_ALL),
        name="covariance",
    )(jnp.stack([lax.div(s, tile) for s in starts]).astype(jnp.int32), *args)


def per_device(nd, na, factors, returns):
    reps = na // nd
    depth, width = returns.shape
    days = depth * nd
    xor = nd & (nd - 1) == 0

    def mix(i, k, j):
        return i ^ k ^ j if xor else (i + k + j) % nd

    def move(x, target):
        pairs = []
        for d in range(nd):
            for a in range(na):
                to = target(d, a // reps, a % reps)
                pairs.append((d * na + a, to[0] * na + to[1] * reps + to[2]))
        return lax.ppermute(x, AXES, pairs)

    def shift(i, j):
        return i ^ j if xor else (i + j) % nd

    def unshift(i, j):
        return i ^ j if xor else (i - j + nd) % nd

    d = lax.axis_index("days")
    a = lax.axis_index("assets")
    q, c = lax.div(a, reps), lax.rem(a, reps)
    order = jnp.stack([unshift(d, j) for j in range(nd)]).astype(jnp.int32)
    col_order = jnp.stack([mix(q, d, j) if xor else (q - d - j + 2 * nd) % nd for j in range(nd)]).astype(jnp.int32)

    def plane(x, j):
        return move(x, lambda d, q, c: (shift(d, j), q, c))

    factor_pieces = [factors] + [plane(factors, j) for j in range(1, nd)]
    row_pieces = [returns] + [plane(returns, j) for j in range(1, nd)]

    sizes = [width * s // sum(CHUNKS) for s in CHUNKS]
    starts = [sum(sizes[:i]) for i in range(len(sizes))]
    top = nd // 2 if xor and nd > 1 else 0
    chunk_pieces = []
    for start, size in zip(starts, sizes):
        x = lax.optimization_barrier(returns[:, start : start + size])
        if top:
            far = move(x, lambda d, q, c: (d, q ^ top, c))
            flip = (d & top) != 0
            sends = [jnp.where(flip, far, x), jnp.where(flip, x, far)]
        pieces = []
        for j in range(nd):
            if top:
                target = lambda d, q, c, j=j: (q ^ ((d ^ j) & top), q ^ ((d ^ j) & ~top), c)
                pieces.append(move(sends[1 if j & top else 0], target))
            else:
                pieces.append(move(x, lambda d, q, c, j=j: (q, mix(q, d, j), c)))
        chunk_pieces.append(pieces)

    full, high, low = invert(order, factor_pieces)
    rows, loadings = residuals(order, row_pieces, high, low, full, width, True)

    held = None
    total = reps * width
    for i, (start, pieces) in enumerate(zip(starts, chunk_pieces)):
        (cols,) = residuals(col_order, pieces, high, low, full, sizes[i], False)
        parts, at = [], []
        for s in range(reps):
            parts.append(cols if s == 0 else move(cols, lambda d, q, c: (d, q, (c - s) % reps)))
            at.append(lax.rem(c + s, reps) * width + start)
        last = i == len(sizes) - 1
        groups = [[s] for s in range(reps)] if last else [list(range(reps))]
        for group in groups:
            held = covariance(held, rows, [parts[s] for s in group], [at[s] for s in group], total, days)
    return loadings, held


def solution(mesh):
    nd, na = mesh.shape["days"], mesh.shape["assets"]

    def body(factors, returns):
        return per_device(nd, na, factors, returns)

    return jax.shard_map(
        body,
        mesh=mesh,
        in_specs=(P("days", None), P("days", "assets")),
        out_specs=(P(None, "assets"), P("assets", "days")),
        check_vma=False,
    )
```

```python
import functools

import jax
import jax.numpy as jnp
from jax import lax
from jax.experimental import pallas as pl
from jax.experimental.pallas import tpu as pltpu
from jax.sharding import PartitionSpec as P


AXES = ("days", "assets")
NB = 64
STEPS = 24
CHUNKS = (1, 1)
BF, F32 = jnp.bfloat16, jnp.float32
VMEM_ALL = 67043328
HIGHEST = lax.Precision.HIGHEST


def dot(a, b, dims=((1,), (0,)), precision=None):
    return lax.dot_general(a, b, (dims, ((), ())), precision=precision, preferred_element_type=F32)


def cost(flops, nbytes):
    return pl.CostEstimate(flops=int(flops), bytes_accessed=int(nbytes), transcendentals=0)


def small_inverse(block):
    n = block.shape[0]
    row = lax.broadcasted_iota(jnp.int32, (n, n), 0)
    col = lax.broadcasted_iota(jnp.int32, (n, n), 1)
    for k in range(n):
        pivot = 1.0 / block[k : k + 1, k : k + 1]
        r = jnp.where(col[:1] == k, 1.0, block[k : k + 1, :]) * pivot
        c = jnp.where(row[:, :1] == k, -1.0, block[:, k : k + 1])
        block = jnp.where((row == k) | (col == k), 0.0, block) - c * r
    return block


def sweep(a, b):
    size = a.shape[0]
    lo, hi = b * NB, (b + 1) * NB
    wide = lambda shape, axis: lax.broadcasted_iota(jnp.int32, shape, axis)
    inverse = small_inverse(a[lo:hi, lo:hi])
    across = wide((NB, size), 1) - lo
    unit = jnp.where(wide((NB, size), 0) == across, 1.0, 0.0)
    across = dot(inverse, jnp.where((across >= 0) & (across < NB), unit, a[lo:hi, :]), precision=HIGHEST)
    rows = wide((size, NB), 0) - lo
    unit = jnp.where(rows == wide((size, NB), 1), -1.0, 0.0)
    down = jnp.where((rows >= 0) & (rows < NB), unit, a[:, lo:hi])
    row, col = wide((size, size), 0), wide((size, size), 1)
    inside = ((row >= lo) & (row < hi)) | ((col >= lo) & (col < hi))
    a[...] = jnp.where(inside, 0.0, a[...]) - dot(down, across, precision=HIGHEST)


def split(a):
    high = a.astype(BF)
    return high, (a - high.astype(F32)).astype(BF)


def dot3(a, b):
    return dot(a[0], b[0]) + dot(a[0], b[1]) + dot(a[1], b[0])


def invert_kernel(n, order, *refs):
    pieces = refs[:n]
    full, high, low, gram, x = refs[n:]
    depth, size = pieces[0].shape
    for j in range(n):
        full[pl.ds(pl.multiple_of(order[j] * depth, depth), depth), :] = pieces[j][...]
    gram[...] = dot(full[...], full[...], ((0,), (0,)))

    parts = split(gram[...])
    row = lax.broadcasted_iota(jnp.int32, (size, size), 0)
    col = lax.broadcasted_iota(jnp.int32, (size, size), 1)
    eye = jnp.where(row == col, 1.0, 0.0)
    bound = jnp.max(jnp.sum(jnp.abs(gram[...]), axis=0, keepdims=True), axis=1, keepdims=True)
    x[...] = eye * (1.0 / bound)

    def step():
        at = split(x[...])
        rest = eye - dot3(parts, at)
        x[...] = x[...] + dot3(at, split(rest))
        return rest

    for _ in range(4):
        step()

    def body(carry):
        rest = step()
        return carry[0] + 1, jnp.sum(rest * rest)

    def going(carry):
        return (carry[0] < STEPS) & jnp.logical_not(carry[1] < 1e-4)

    _, error = lax.while_loop(going, body, (0, jnp.float32(1.0)))
    done = error < 1e-4

    @pl.when(done)
    def _():
        rest = eye - dot(gram[...], x[...], precision=HIGHEST)
        x[...] = x[...] + dot(x[...], rest, precision=HIGHEST)

    @pl.when(jnp.logical_not(done))
    def _():
        x[...] = gram[...]
        for b in range(size // NB):
            sweep(x, b)

    h = dot(x[...], full[...].astype(F32), ((1,), (1,)), precision=HIGHEST)
    high[...], low[...] = split(h)


def invert(order, pieces):
    n = len(pieces)
    depth, size = pieces[0].shape
    days = n * depth
    return pl.pallas_call(
        functools.partial(invert_kernel, n),
        in_specs=[pl.BlockSpec(memory_space=pltpu.SMEM)] + [pl.BlockSpec(memory_space=pltpu.VMEM)] * n,
        out_shape=[jax.ShapeDtypeStruct((days, size), BF)] + [jax.ShapeDtypeStruct((size, days), BF)] * 2,
        scratch_shapes=[pltpu.VMEM((size, size), F32)] * 2,
        cost_estimate=cost(2e10, 8 * days * size),
        compiler_params=pltpu.CompilerParams(vmem_limit_bytes=VMEM_ALL),
        name="gram",
    )(order, *pieces)


def residual_kernel(slots, depth, with_loadings, order, *refs):
    count = len(slots)
    high, low, factors = refs[count : count + 3]
    outs = refs[count + 3 : -1]
    y = refs[-1]
    for (j, offset), ref in zip(slots, refs[:count]):
        rows = ref.shape[0]
        at = pl.multiple_of(order[j] * depth, depth) + offset
        y[pl.ds(pl.multiple_of(at, rows), rows), :] = ref[...]
    loadings = dot(high[...], y[...]) + dot(low[...], y[...])
    fitted = dot(factors[...], loadings.astype(BF))
    outs[0][...] = (y[...].astype(F32) - fitted).astype(BF)
    if with_loadings:
        outs[1][...] = loadings


def residuals(order, pieces, slots, high, low, factors, width, with_loadings, tile=1024):
    size, days = high.shape
    depth = days // order.shape[0]
    tile = min(tile, width)
    whole = lambda shape: pl.BlockSpec(shape, lambda i, order: (0, 0))
    specs = [pl.BlockSpec((p.shape[0], tile), lambda i, order: (0, i)) for p in pieces]
    out_specs = [pl.BlockSpec((days, tile), lambda i, order: (0, i))]
    out_shape = [jax.ShapeDtypeStruct((days, width), BF)]
    if with_loadings:
        out_specs.append(pl.BlockSpec((size, tile), lambda i, order: (0, i)))
        out_shape.append(jax.ShapeDtypeStruct((size, width), F32))
    return pl.pallas_call(
        functools.partial(residual_kernel, slots, depth, with_loadings),
        grid_spec=pltpu.PrefetchScalarGridSpec(
            num_scalar_prefetch=1,
            grid=(width // tile,),
            in_specs=specs + [whole((size, days))] * 2 + [whole((days, size))],
            out_specs=out_specs,
            scratch_shapes=[pltpu.VMEM((days, tile), BF)],
        ),
        out_shape=out_shape,
        cost_estimate=cost(6 * days * size * width, 4 * days * width),
        compiler_params=pltpu.CompilerParams(vmem_limit_bytes=VMEM_ALL),
        name="residual",
    )(order, *pieces, high, low, factors)


def covariance_kernel(scale, count, where, rows, *refs):
    out = refs[-1]
    step = pl.program_id(0)
    for k in range(count):
        @pl.when(step == k if count > 1 else step >= 0)
        def _():
            out[...] = dot(rows[...], refs[k][...], ((0,), (0,))) * scale


def covariance(held, rows, parts, starts, total, days, tile=512):
    depth, height = rows.shape
    width = parts[0].shape[1]
    tile = min(tile, width)
    count, tiles = len(parts), width // tile
    specs = [pl.BlockSpec((depth, height), lambda k, j, where: (0, 0))]
    for k in range(count):
        held_at = lambda s, j, where, k=k: (0, jnp.where(s == k, j, jnp.where(s < k, 0, tiles - 1)))
        specs.append(pl.BlockSpec((depth, tile), held_at))
    args = [rows, *parts]
    aliases = {}
    if held is not None:
        specs.append(pl.BlockSpec(memory_space=pl.ANY))
        args.append(held)
        aliases = {len(args): 0}
    return pl.pallas_call(
        functools.partial(covariance_kernel, 1.0 / days, count),
        grid_spec=pltpu.PrefetchScalarGridSpec(
            num_scalar_prefetch=1,
            grid=(count, tiles),
            in_specs=specs,
            out_specs=pl.BlockSpec((height, tile), lambda k, j, where: (0, where[k] + j)),
        ),
        out_shape=jax.ShapeDtypeStruct((height, total), F32),
        input_output_aliases=aliases,
        cost_estimate=cost(2 * depth * height * width * count, 4 * height * width * count),
        compiler_params=pltpu.CompilerParams(vmem_limit_bytes=VMEM_ALL),
        name="covariance",
    )(jnp.stack([lax.div(s, tile) for s in starts]).astype(jnp.int32), *args)


def relayed(nd):
    return nd == 4


def per_device(nd, na, factors, returns):
    reps = na // nd
    depth, width = returns.shape
    days = depth * nd
    xor = nd & (nd - 1) == 0

    def mix(i, k, j):
        return i ^ k ^ j if xor else (i + k + j) % nd

    def move(x, target):
        pairs = []
        for d in range(nd):
            for a in range(na):
                to = target(d, a // reps, a % reps)
                pairs.append((d * na + a, to[0] * na + to[1] * reps + to[2]))
        return lax.ppermute(x, AXES, pairs)

    def shift(i, j):
        return i ^ j if xor else (i + j) % nd

    def unshift(i, j):
        return i ^ j if xor else (i - j + nd) % nd

    d = lax.axis_index("days")
    a = lax.axis_index("assets")
    q, c = lax.div(a, reps), lax.rem(a, reps)
    order = jnp.stack([unshift(d, j) for j in range(nd)]).astype(jnp.int32)
    col_order = jnp.stack([mix(q, d, j) if xor else (q - d - j + 2 * nd) % nd for j in range(nd)]).astype(jnp.int32)

    def plane(x, j):
        return move(x, lambda d, q, c: (shift(d, j), q, c))

    factor_pieces = [factors] + [plane(factors, j) for j in range(1, nd)]
    slots = [(j, 0) for j in range(nd)]
    if relayed(nd):
        half = depth // 2
        one, two = plane(returns, 1), plane(returns, 2)
        upper = one[:half]
        lower = two[half:]
        row_pieces = [returns, one, two, plane(upper, 2), plane(lower, 1)]
        row_slots = slots[:3] + [(3, 0), (3, half)]
    else:
        row_pieces = [returns] + [plane(returns, j) for j in range(1, nd)]
        row_slots = slots

    sizes = [width * s // sum(CHUNKS) for s in CHUNKS]
    starts = [sum(sizes[:i]) for i in range(len(sizes))]
    top = nd // 2 if xor and nd > 1 else 0
    chunk_pieces = []
    for start, size in zip(starts, sizes):
        x = lax.optimization_barrier(returns[:, start : start + size])
        if top:
            far = move(x, lambda d, q, c: (d, q ^ top, c))
            flip = (d & top) != 0
            sends = [jnp.where(flip, far, x), jnp.where(flip, x, far)]
        pieces = []
        for j in range(nd):
            if top:
                target = lambda d, q, c, j=j: (q ^ ((d ^ j) & top), q ^ ((d ^ j) & ~top), c)
                pieces.append(move(sends[1 if j & top else 0], target))
            else:
                pieces.append(move(x, lambda d, q, c, j=j: (q, mix(q, d, j), c)))
        chunk_pieces.append(pieces)

    full, high, low = invert(order, factor_pieces)
    rows, loadings = residuals(order, row_pieces, row_slots, high, low, full, width, True)

    held = None
    total = reps * width
    for i, (start, pieces) in enumerate(zip(starts, chunk_pieces)):
        (cols,) = residuals(col_order, pieces, slots, high, low, full, sizes[i], False)
        parts, at = [], []
        for s in range(reps):
            parts.append(cols if s == 0 else move(cols, lambda d, q, c: (d, q, (c - s) % reps)))
            at.append(lax.rem(c + s, reps) * width + start)
        last = i == len(sizes) - 1
        groups = [[s] for s in range(reps)] if last else [list(range(reps))]
        for group in groups:
            held = covariance(held, rows, [parts[s] for s in group], [at[s] for s in group], total, days)
    return loadings, held


def solution(mesh):
    nd, na = mesh.shape["days"], mesh.shape["assets"]

    def body(factors, returns):
        return per_device(nd, na, factors, returns)

    return jax.shard_map(
        body,
        mesh=mesh,
        in_specs=(P("days", None), P("days", "assets")),
        out_specs=(P(None, "assets"), P("assets", "days")),
        check_vma=False,
    )
```

```python
import functools

import jax
import jax.numpy as jnp
from jax import lax
from jax.experimental import pallas as pl
from jax.experimental.pallas import tpu as pltpu
from jax.sharding import PartitionSpec as P


AXES = ("days", "assets")
NB = 64
STEPS = 24
CHUNKS = (1, 1)
BF, F32 = jnp.bfloat16, jnp.float32
VMEM_ALL = 67043328
VMEM_MOST = 54525952
VMEM_SOME = 33554432
HIGHEST = lax.Precision.HIGHEST


def dot(a, b, dims=((1,), (0,)), precision=None):
    return lax.dot_general(a, b, (dims, ((), ())), precision=precision, preferred_element_type=F32)


def cost(flops, nbytes):
    return pl.CostEstimate(flops=int(flops), bytes_accessed=int(nbytes), transcendentals=0)


def small_inverse(block):
    n = block.shape[0]
    row = lax.broadcasted_iota(jnp.int32, (n, n), 0)
    col = lax.broadcasted_iota(jnp.int32, (n, n), 1)
    for k in range(n):
        pivot = 1.0 / block[k : k + 1, k : k + 1]
        r = jnp.where(col[:1] == k, 1.0, block[k : k + 1, :]) * pivot
        c = jnp.where(row[:, :1] == k, -1.0, block[:, k : k + 1])
        block = jnp.where((row == k) | (col == k), 0.0, block) - c * r
    return block


def sweep(a, b):
    size = a.shape[0]
    lo, hi = b * NB, (b + 1) * NB
    wide = lambda shape, axis: lax.broadcasted_iota(jnp.int32, shape, axis)
    inverse = small_inverse(a[lo:hi, lo:hi])
    across = wide((NB, size), 1) - lo
    unit = jnp.where(wide((NB, size), 0) == across, 1.0, 0.0)
    across = dot(inverse, jnp.where((across >= 0) & (across < NB), unit, a[lo:hi, :]), precision=HIGHEST)
    rows = wide((size, NB), 0) - lo
    unit = jnp.where(rows == wide((size, NB), 1), -1.0, 0.0)
    down = jnp.where((rows >= 0) & (rows < NB), unit, a[:, lo:hi])
    row, col = wide((size, size), 0), wide((size, size), 1)
    inside = ((row >= lo) & (row < hi)) | ((col >= lo) & (col < hi))
    a[...] = jnp.where(inside, 0.0, a[...]) - dot(down, across, precision=HIGHEST)


def split(a):
    high = a.astype(BF)
    return high, (a - high.astype(F32)).astype(BF)


def dot3(a, b):
    return dot(a[0], b[0]) + dot(a[0], b[1]) + dot(a[1], b[0])


def invert_kernel(n, order, *refs):
    pieces = refs[:n]
    full, high, low, gram, x = refs[n:]
    depth, size = pieces[0].shape
    for j in range(n):
        full[pl.ds(pl.multiple_of(order[j] * depth, depth), depth), :] = pieces[j][...]
    gram[...] = dot(full[...], full[...], ((0,), (0,)))

    parts = split(gram[...])
    row = lax.broadcasted_iota(jnp.int32, (size, size), 0)
    col = lax.broadcasted_iota(jnp.int32, (size, size), 1)
    eye = jnp.where(row == col, 1.0, 0.0)
    bound = jnp.max(jnp.sum(jnp.abs(gram[...]), axis=0, keepdims=True), axis=1, keepdims=True)
    x[...] = eye * (1.0 / bound)

    def step():
        at = split(x[...])
        rest = eye - dot3(parts, at)
        x[...] = x[...] + dot3(at, split(rest))
        return rest

    for _ in range(4):
        step()

    def body(carry):
        rest = step()
        return carry[0] + 1, jnp.sum(rest * rest)

    def going(carry):
        return (carry[0] < STEPS) & jnp.logical_not(carry[1] < 1e-4)

    _, error = lax.while_loop(going, body, (0, jnp.float32(1.0)))
    done = error < 1e-4

    @pl.when(done)
    def _():
        rest = eye - dot(gram[...], x[...], precision=HIGHEST)
        x[...] = x[...] + dot(x[...], rest, precision=HIGHEST)

    @pl.when(jnp.logical_not(done))
    def _():
        x[...] = gram[...]
        for b in range(size // NB):
            sweep(x, b)

    h = dot(x[...], full[...].astype(F32), ((1,), (1,)), precision=HIGHEST)
    high[...], low[...] = split(h)


def invert(order, pieces):
    n = len(pieces)
    depth, size = pieces[0].shape
    days = n * depth
    return pl.pallas_call(
        functools.partial(invert_kernel, n),
        in_specs=[pl.BlockSpec(memory_space=pltpu.SMEM)] + [pl.BlockSpec(memory_space=pltpu.VMEM)] * n,
        out_shape=[jax.ShapeDtypeStruct((days, size), BF)] + [jax.ShapeDtypeStruct((size, days), BF)] * 2,
        scratch_shapes=[pltpu.VMEM((size, size), F32)] * 2,
        cost_estimate=cost(2e10, 8 * days * size),
        compiler_params=pltpu.CompilerParams(vmem_limit_bytes=VMEM_ALL),
        name="gram",
    )(order, *pieces)


def residual_kernel(slots, depth, with_loadings, order, *refs):
    count = len(slots)
    high, low, factors = refs[count : count + 3]
    outs = refs[count + 3 : -1]
    y = refs[-1]
    for (j, offset), ref in zip(slots, refs[:count]):
        rows = ref.shape[0]
        at = pl.multiple_of(order[j] * depth, depth) + offset
        y[pl.ds(pl.multiple_of(at, rows), rows), :] = ref[...]
    loadings = dot(high[...], y[...]) + dot(low[...], y[...])
    fitted = dot(factors[...], loadings.astype(BF))
    outs[0][...] = (y[...].astype(F32) - fitted).astype(BF)
    if with_loadings:
        outs[1][...] = loadings


def residuals(order, pieces, slots, high, low, factors, width, with_loadings, tile=1024):
    size, days = high.shape
    depth = days // order.shape[0]
    tile = min(tile, width)
    specs = [pl.BlockSpec((p.shape[0], tile), lambda i, order: (0, i)) for p in pieces]
    out_specs = [pl.BlockSpec((days, tile), lambda i, order: (0, i))]
    out_shape = [jax.ShapeDtypeStruct((days, width), BF)]
    if with_loadings:
        out_specs.append(pl.BlockSpec((size, tile), lambda i, order: (0, i)))
        out_shape.append(jax.ShapeDtypeStruct((size, width), F32))
    return pl.pallas_call(
        functools.partial(residual_kernel, slots, depth, with_loadings),
        grid_spec=pltpu.PrefetchScalarGridSpec(
            num_scalar_prefetch=1,
            grid=(width // tile,),
            in_specs=specs + [pl.BlockSpec(memory_space=pltpu.VMEM)] * 3,
            out_specs=out_specs,
            scratch_shapes=[pltpu.VMEM((days, tile), BF)],
        ),
        out_shape=out_shape,
        cost_estimate=cost(6 * days * size * width, 4 * days * width),
        compiler_params=pltpu.CompilerParams(vmem_limit_bytes=VMEM_MOST),
        name="residual",
    )(order, *pieces, high, low, factors)


def covariance_kernel(scale, count, where, rows, *refs):
    out = refs[-1]
    step = pl.program_id(0)
    for k in range(count):
        @pl.when(step == k if count > 1 else step >= 0)
        def _():
            out[...] = dot(rows[...], refs[k][...], ((0,), (0,))) * scale


def covariance(held, rows, parts, starts, total, days, tile=512):
    depth, height = rows.shape
    width = parts[0].shape[1]
    tile = min(tile, width)
    count, tiles = len(parts), width // tile
    specs = [pl.BlockSpec(memory_space=pltpu.VMEM)]
    for k in range(count):
        held_at = lambda s, j, where, k=k: (0, jnp.where(s == k, j, jnp.where(s < k, 0, tiles - 1)))
        specs.append(pl.BlockSpec((depth, tile), held_at))
    args = [rows, *parts]
    aliases = {}
    if held is not None:
        specs.append(pl.BlockSpec(memory_space=pl.ANY))
        args.append(held)
        aliases = {len(args): 0}
    return pl.pallas_call(
        functools.partial(covariance_kernel, 1.0 / days, count),
        grid_spec=pltpu.PrefetchScalarGridSpec(
            num_scalar_prefetch=1,
            grid=(count, tiles),
            in_specs=specs,
            out_specs=pl.BlockSpec((height, tile), lambda k, j, where: (0, where[k] + j)),
        ),
        out_shape=jax.ShapeDtypeStruct((height, total), F32),
        input_output_aliases=aliases,
        cost_estimate=cost(2 * depth * height * width * count, 4 * height * width * count),
        compiler_params=pltpu.CompilerParams(vmem_limit_bytes=VMEM_SOME),
        name="covariance",
    )(jnp.stack([lax.div(s, tile) for s in starts]).astype(jnp.int32), *args)


def relayed(nd):
    return nd == 4


def per_device(nd, na, factors, returns):
    reps = na // nd
    depth, width = returns.shape
    days = depth * nd
    xor = nd & (nd - 1) == 0

    def mix(i, k, j):
        return i ^ k ^ j if xor else (i + k + j) % nd

    def move(x, target):
        pairs = []
        for d in range(nd):
            for a in range(na):
                to = target(d, a // reps, a % reps)
                pairs.append((d * na + a, to[0] * na + to[1] * reps + to[2]))
        return lax.ppermute(x, AXES, pairs)

    def shift(i, j):
        return i ^ j if xor else (i + j) % nd

    def unshift(i, j):
        return i ^ j if xor else (i - j + nd) % nd

    d = lax.axis_index("days")
    a = lax.axis_index("assets")
    q, c = lax.div(a, reps), lax.rem(a, reps)
    order = jnp.stack([unshift(d, j) for j in range(nd)]).astype(jnp.int32)
    col_order = jnp.stack([mix(q, d, j) if xor else (q - d - j + 2 * nd) % nd for j in range(nd)]).astype(jnp.int32)

    def plane(x, j):
        return move(x, lambda d, q, c: (shift(d, j), q, c))

    factor_pieces = [factors] + [plane(factors, j) for j in range(1, nd)]
    slots = [(j, 0) for j in range(nd)]
    if relayed(nd):
        half = depth // 2
        one, two = plane(returns, 1), plane(returns, 2)
        upper = one[:half]
        lower = two[half:]
        row_pieces = [returns, one, two, plane(upper, 2), plane(lower, 1)]
        row_slots = slots[:3] + [(3, 0), (3, half)]
    else:
        row_pieces = [returns] + [plane(returns, j) for j in range(1, nd)]
        row_slots = slots

    sizes = [width * s // sum(CHUNKS) for s in CHUNKS]
    starts = [sum(sizes[:i]) for i in range(len(sizes))]
    top = nd // 2 if xor and nd > 1 else 0
    chunk_pieces = []
    for start, size in zip(starts, sizes):
        x = lax.optimization_barrier(returns[:, start : start + size])
        if top:
            far = move(x, lambda d, q, c: (d, q ^ top, c))
            flip = (d & top) != 0
            sends = [jnp.where(flip, far, x), jnp.where(flip, x, far)]
        pieces = []
        for j in range(nd):
            if top:
                target = lambda d, q, c, j=j: (q ^ ((d ^ j) & top), q ^ ((d ^ j) & ~top), c)
                pieces.append(move(sends[1 if j & top else 0], target))
            else:
                pieces.append(move(x, lambda d, q, c, j=j: (q, mix(q, d, j), c)))
        chunk_pieces.append(pieces)

    full, high, low = invert(order, factor_pieces)
    rows, loadings = residuals(order, row_pieces, row_slots, high, low, full, width, True)

    held = None
    total = reps * width
    for i, (start, pieces) in enumerate(zip(starts, chunk_pieces)):
        (cols,) = residuals(col_order, pieces, slots, high, low, full, sizes[i], False)
        parts, at = [], []
        for s in range(reps):
            parts.append(cols if s == 0 else move(cols, lambda d, q, c: (d, q, (c - s) % reps)))
            at.append(lax.rem(c + s, reps) * width + start)
        last = i == len(sizes) - 1
        groups = [[s] for s in range(reps)] if last else [list(range(reps))]
        for group in groups:
            held = covariance(held, rows, [parts[s] for s in group], [at[s] for s in group], total, days)
    return loadings, held


def solution(mesh):
    nd, na = mesh.shape["days"], mesh.shape["assets"]

    def body(factors, returns):
        return per_device(nd, na, factors, returns)

    return jax.shard_map(
        body,
        mesh=mesh,
        in_specs=(P("days", None), P("days", "assets")),
        out_specs=(P(None, "assets"), P("assets", "days")),
        check_vma=False,
    )
```
